32 devices in a mesh: groups: 2 (over x), ctx: 16 (over z, y, core).
Axes of the slice: x: 2, y: 2, z: 4, core: 2. Of those that a mesh axis runs over, the one named last changes fastest.
Arguments:
- queries: bfloat16 [16384, 3584], P(('groups', 'ctx')), parts along dimension 0, may hold values from -48 to 48
- keys: bfloat16 [16384, 512], P(('groups', 'ctx')), parts along dimension 0, may hold values from -6 to 6
- values: bfloat16 [16384, 512], P(('groups', 'ctx')), parts along dimension 0, may hold values from -6 to 6
- out_grad: bfloat16 [16384, 3584], P(('groups', 'ctx')), parts along dimension 0, may hold values from -6 to 6
- links: int32 [128, 4], P(('groups', 'ctx')), parts along dimension 0, may hold values from -1 to 3, as said below
- header_blocks: int32 [8], P('groups'), parts along dimension 0, may hold values from 0 to 59, as said below
Outputs:
- query_grad: bfloat16 [16384, 3584], P(('groups', 'ctx')), parts along dimension 0
- key_gradient_array: float32 [16384, 512], P(('groups', 'ctx')), parts along dimension 0
- value_gradient_array: float32 [16384, 512], P(('groups', 'ctx')), parts along dimension 0
The draws below stay inside these ranges and needn't reach their ends.
There are 2 independent parts, one for each index of `groups`. The reference program is written for one: setup_inputs(seed, part) draws one part's arguments, and reference() takes and returns one part's arrays. A program takes and returns all parts, laid end to end along the dimension named above; each array names one. Nothing has to cross between parts.
Inputs may be any that keep to these rules, and one draw needn't show every extreme that they name: `header_blocks`: strictly increasing; no two header blocks lie among the same aligned 4 blocks, and none lies among the last 4 blocks. Non-empty entries of one row are distinct header numbers whose header block ends before the row's window part begins (header_blocks[links[b, l]] <= b - 256 / 128 - 1). The last row has no empty entry.
All inputs are finite; a program needn't handle non-finite values.
Results may differ from the reference program's by a relative error of at most 0.012.
Values may be sent and summed in bfloat16 or wider, within the bound.
A program may use at most 192 MiB of HBM per device.

```python
import jax
import jax.numpy as jnp
from jax import lax

QUERY_HEADS = 28
KEY_VALUE_HEADS = 4
HEAD_SIZE = 128
BLK = 128
WIN = 256
LINKS = 4
BLK_DEV = 4
SEQUENCE_SPAN = 8192
NQB = 64
NH = 4


def query_key_pair(key):
    query_key = jax.random.fold_in(key, 11)
    key_lookup_name = jax.random.fold_in(key, 12)
    query_out = jnp.clip(jax.random.normal(query_key, (SEQUENCE_SPAN, QUERY_HEADS * HEAD_SIZE), jnp.float32), -6.0, 6.0)
    key_result_output = jnp.clip(jax.random.normal(key_lookup_name, (SEQUENCE_SPAN, KEY_VALUE_HEADS * HEAD_SIZE), jnp.float32), -6.0, 6.0)
    return (query_out, key_result_output)


def draw_queries(key, part):
    return query_key_pair(key)[0].astype(jnp.bfloat16)


def draw_keys(key, part):
    return query_key_pair(key)[1].astype(jnp.bfloat16)


def header_layout(key):
    base = jax.random.fold_in(key, 21)
    device_count = NQB // BLK_DEV
    middle = jax.random.permutation(jax.random.fold_in(base, 1), device_count - 3)[:NH - 2].astype(jnp.int32) + 1
    owners = jnp.sort(jnp.concatenate([jnp.zeros((1,), jnp.int32), middle, jnp.full((1,), device_count - 2, jnp.int32)]))
    offsets = jax.random.randint(jax.random.fold_in(base, 2), (NH,), 0, BLK_DEV).astype(jnp.int32)
    offsets = offsets.at[0].set(0).at[NH - 1].set(BLK_DEV - 1)
    return (owners * BLK_DEV + offsets).astype(jnp.int32)


def draw_header_blocks(key, part):
    return header_layout(key)


def draw_links(key, part):
    blocks = header_layout(key)
    base = jax.random.fold_in(key, 31)
    row_ids = jnp.arange(NQB, dtype=jnp.int32)
    slot_ids = jnp.arange(NH, dtype=jnp.int32)
    eligible = blocks[None, :] <= row_ids[:, None] - WIN // BLK - 1
    noise = jax.random.randint(jax.random.fold_in(base, 1), (NQB, NH), 0, 1 << 16).astype(jnp.int32)
    score = noise * NH + slot_ids[None, :]
    forced = (row_ids[:, None] == NQB - 1) & (slot_ids[None, :] == NH - 1)
    score = score + eligible.astype(jnp.int32) * (1 << 25) + forced.astype(jnp.int32) * (1 << 24)
    ignored, chosen = lax.top_k(score, LINKS)
    density = jax.random.randint(jax.random.fold_in(base, 2), (NQB // BLK_DEV,), 0, LINKS + 1).astype(jnp.int32)
    row_cap = jnp.repeat(density, BLK_DEV)
    counts = jax.random.randint(jax.random.fold_in(base, 3), (NQB,), 0, row_cap + 1).astype(jnp.int32)
    counts = jnp.where(row_ids == NQB - 1, LINKS, counts)
    usable = jnp.take_along_axis(eligible, chosen, axis=1)
    keep_entry = (jnp.arange(LINKS, dtype=jnp.int32)[None, :] < counts[:, None]) & usable
    return jnp.where(keep_entry, chosen, -1).astype(jnp.int32)


def levels(own_key, dims, split, low, high):
    factor_of, own = 1.0, jax.random.fold_in(own_key, 6)
    for axis_at, parts in split:
        draws = jnp.exp(jax.random.uniform(jax.random.fold_in(own, axis_at), (parts,), jnp.float32, low / len(split), high / len(split)))
        factor_of = factor_of * jnp.repeat(draws, dims[axis_at] // parts).reshape([-1 if axis == axis_at else 1 for axis in range(len(dims))])
    return factor_of


def centred(rng, extent, scale, limit, cuts=(), kind=jnp.bfloat16):
    values = scale * jax.random.normal(rng, extent, jnp.float32)
    if cuts:
        values = values * levels(rng, extent, cuts, -0.22, 0.18)
    return jnp.clip(values, -limit, limit).astype(kind)


def setup_inputs(seed: int = 0, part: int = 0) -> dict:
    key_list = jax.random.split(jax.random.key(seed), 7)
    part_splits = jax.random.split(jax.random.fold_in(key_list[6], part), 7)
    return {
        "queries": draw_queries(jax.random.fold_in(jax.random.fold_in(key_list[6], part), 71), part),
        "keys": draw_keys(jax.random.fold_in(jax.random.fold_in(key_list[6], part), 71), part),
        "values": centred(part_splits[2], (SEQUENCE_SPAN, KEY_VALUE_HEADS * HEAD_SIZE), 1.0, 6.0, ((0, 16),)),
        "out_grad": centred(part_splits[3], (SEQUENCE_SPAN, QUERY_HEADS * HEAD_SIZE), 1.0, 6.0, ((0, 16),)),
        "links": draw_links(jax.random.fold_in(jax.random.fold_in(key_list[6], part), 71), part),
        "header_blocks": draw_header_blocks(jax.random.fold_in(jax.random.fold_in(key_list[6], part), 71), part),
    }


def block_grads(query_row_block, gradient_row_block, key_row_block, value_row_block, is_valid):
    row_total_count = query_row_block.shape[0]
    key_total_count = key_row_block.shape[0]
    queries_each_group = QUERY_HEADS // KEY_VALUE_HEADS
    factor = float(HEAD_SIZE) ** -0.5
    highest = lax.Precision.HIGHEST
    query_four_axes = query_row_block.astype(jnp.float32).reshape(row_total_count, KEY_VALUE_HEADS, queries_each_group, HEAD_SIZE)
    gradient_four_axes = gradient_row_block.astype(jnp.float32).reshape(row_total_count, KEY_VALUE_HEADS, queries_each_group, HEAD_SIZE)
    key_three_axes = key_row_block.astype(jnp.float32).reshape(key_total_count, KEY_VALUE_HEADS, HEAD_SIZE)
    value_three_axes = value_row_block.astype(jnp.float32).reshape(key_total_count, KEY_VALUE_HEADS, HEAD_SIZE)
    scores = jnp.einsum("qgrd,kgd->gqrk", query_four_axes, key_three_axes, precision=highest) * factor
    scores = jnp.where(is_valid[None, :, None, :], scores, -1e30)
    row_max = jnp.max(scores, axis=-1, keepdims=True)
    weights = jnp.exp(scores - row_max)
    attend = weights / jnp.sum(weights, axis=-1, keepdims=True)
    d_attend = jnp.einsum("qgrd,kgd->gqrk", gradient_four_axes, value_three_axes, precision=highest)
    row_delta = jnp.sum(attend * d_attend, axis=-1, keepdims=True)
    d_scores = (attend * (d_attend - row_delta) * factor).astype(jnp.bfloat16).astype(jnp.float32)
    attend_low = attend.astype(jnp.bfloat16).astype(jnp.float32)
    query_grad = jnp.einsum("gqrk,kgd->qgrd", d_scores, key_three_axes, precision=highest)
    key_gradient_array = jnp.einsum("gqrk,qgrd->kgd", d_scores, query_four_axes, precision=highest)
    value_gradient_array = jnp.einsum("gqrk,qgrd->kgd", attend_low, gradient_four_axes, precision=highest)
    key_value_gradient = jnp.concatenate([key_gradient_array.reshape(key_total_count, KEY_VALUE_HEADS * HEAD_SIZE), value_gradient_array.reshape(key_total_count, KEY_VALUE_HEADS * HEAD_SIZE)], axis=1)
    return query_grad.reshape(row_total_count, QUERY_HEADS * HEAD_SIZE), key_value_gradient


def reference(queries, keys, values, out_grad, links, header_blocks):
    seq_len = queries.shape[0]
    block_total = seq_len // BLK
    half_width = keys.shape[1]
    kv_full = jnp.concatenate([keys, values], axis=1)
    kv_width = kv_full.shape[1]
    padded = jnp.concatenate([jnp.zeros((WIN, kv_width), kv_full.dtype), kv_full], axis=0)
    window_span = WIN + BLK

    def one_block(acc, block_id):
        row_start = (block_id * BLK).astype(jnp.int32)
        query_row_block = lax.dynamic_slice_in_dim(queries, row_start, BLK, 0)
        gradient_row_block = lax.dynamic_slice_in_dim(out_grad, row_start, BLK, 0)
        window = lax.dynamic_slice_in_dim(padded, row_start, window_span, 0)
        entries = links[block_id]
        is_live = entries >= 0
        safe_slot = jnp.where(is_live, entries, 0).astype(jnp.int32)
        header_ids = header_blocks[safe_slot].astype(jnp.int32)
        pieces = [lax.dynamic_slice_in_dim(kv_full, (header_ids[slot] * BLK).astype(jnp.int32), BLK, 0) for slot in range(LINKS)]
        key_tile = jnp.concatenate([window] + pieces, axis=0)
        q_pos = row_start + jnp.arange(BLK, dtype=jnp.int32)
        k_pos = row_start - WIN + jnp.arange(window_span, dtype=jnp.int32)
        near_ok = (k_pos[None, :] <= q_pos[:, None]) & (q_pos[:, None] - k_pos[None, :] < WIN) & (k_pos[None, :] >= 0)
        far_ok = jnp.broadcast_to(jnp.repeat(is_live, BLK)[None, :], (BLK, LINKS * BLK))
        is_valid = jnp.concatenate([near_ok, far_ok], axis=1)
        query_grad, key_value_gradient = block_grads(query_row_block, gradient_row_block, key_tile[:, :half_width], key_tile[:, half_width:], is_valid)
        current = lax.dynamic_slice_in_dim(acc, row_start, window_span, 0)
        acc = lax.dynamic_update_slice_in_dim(acc, current + key_value_gradient[:window_span], row_start, 0)
        for slot in range(LINKS):
            target = (WIN + header_ids[slot] * BLK).astype(jnp.int32)
            extra = key_value_gradient[window_span + slot * BLK: window_span + (slot + 1) * BLK] * is_live[slot].astype(jnp.float32)
            current = lax.dynamic_slice_in_dim(acc, target, BLK, 0)
            acc = lax.dynamic_update_slice_in_dim(acc, current + extra, target, 0)
        return acc, query_grad.astype(jnp.bfloat16)

    start_acc = jnp.zeros((seq_len + WIN, kv_width), jnp.float32)
    acc, dq_blocks = lax.scan(one_block, start_acc, jnp.arange(block_total, dtype=jnp.int32))
    query_out = dq_blocks.reshape(seq_len, QUERY_HEADS * HEAD_SIZE)
    full_grad = acc[WIN:]
    return query_out, full_grad[:, :half_width], full_grad[:, half_width:]
```

```python
import functools
import math

import jax
import jax.numpy as jnp
from jax import lax
from jax.experimental import pallas as pl
from jax.experimental.pallas import tpu as pltpu
from jax.sharding import PartitionSpec as P

QUERY_HEADS = 28
KEY_VALUE_HEADS = 4
HEAD_SIZE = 128
BLK = 128
WIN = 256
LINKS = 4
REP = QUERY_HEADS // KEY_VALUE_HEADS
CHUNKS = 2
FACTOR = float(HEAD_SIZE) ** (-0.5)
EXP2_FACTOR = FACTOR * math.log2(math.e)
NT = (((1,), (1,)), ((), ()))


def shifted(x, axis, by):
    peers = lax.axis_size(axis)
    pairs = [(i, i + by) for i in range(peers) if 0 <= i + by < peers]
    return lax.ppermute(x, axis, pairs)


def dot(a, b, dims=(((1,), (0,)), ((), ()))):
    return lax.dot_general(a, b, dims, preferred_element_type=jnp.float32)


def grad_kernel(block_count, links, headers, index, q_ref, o_ref, k_ref, v_ref, hk_ref, hv_ref, prev_ref,
                dq_ref, near_ref, far_ref, kcat, vcat, ds_s, p_s, near_acc, far_acc):
    b = pl.program_id(1)
    first = index[0] * block_count + b
    row = pl.multiple_of(b * BLK, BLK)

    @pl.when(b == 0)
    def _():
        near_acc[...] = jnp.zeros_like(near_acc)
        far_acc[...] = jnp.zeros_like(far_acc)

    kcat[0:3 * BLK] = k_ref[pl.ds(row, 3 * BLK), :]
    vcat[0:3 * BLK] = v_ref[pl.ds(row, 3 * BLK), :]
    live = jnp.int32(0)
    slots = [jnp.int32(0)] * LINKS
    for l in range(LINKS):
        entry = links[b, l]
        holder = headers[jnp.maximum(entry, 0)] // block_count
        for s in range(l + 1):
            slots[s] = jnp.where((entry >= 0) & (live == s), holder, slots[s])
        live = live + jnp.where(entry >= 0, 1, 0).astype(jnp.int32)
    slots = [pl.multiple_of(s * BLK, BLK) for s in slots]

    key_at = lax.broadcasted_iota(jnp.int32, (BLK, BLK), 0)
    query_at = lax.broadcasted_iota(jnp.int32, (BLK, BLK), 1)
    current = key_at <= query_at
    bias0 = jnp.where(first >= 2, 0.0, -1e30).astype(jnp.float32)
    bias1 = jnp.where(first >= 1, 0.0, -1e30).astype(jnp.float32)

    def work(n):
        for s in range(n):
            kcat[(3 + s) * BLK:(4 + s) * BLK] = hk_ref[pl.ds(slots[s], BLK), :]
            vcat[(3 + s) * BLK:(4 + s) * BLK] = hv_ref[pl.ds(slots[s], BLK), :]
        total = (3 + n) * BLK
        for h in range(REP):
            cols = slice(h * HEAD_SIZE, (h + 1) * HEAD_SIZE)
            st = dot(kcat[0:total], q_ref[:, cols], NT)
            dpt = dot(vcat[0:total], o_ref[:, cols], NT)
            x = [jnp.where(current, st[2 * BLK:3 * BLK], st[0:BLK] + bias0), st[BLK:2 * BLK] + bias1]
            d = [jnp.where(current, dpt[2 * BLK:3 * BLK], dpt[0:BLK]), dpt[BLK:2 * BLK]]
            for s in range(n):
                x.append(st[(3 + s) * BLK:(4 + s) * BLK])
                d.append(dpt[(3 + s) * BLK:(4 + s) * BLK])
            top = x[0]
            for t in x[1:]:
                top = jnp.maximum(top, t)
            top = jnp.max(top, axis=0, keepdims=True)
            e = [jnp.exp2((t - top) * EXP2_FACTOR) for t in x]
            norm = e[0]
            mixed = e[0] * d[0]
            for et, dt in zip(e[1:], d[1:]):
                norm = norm + et
                mixed = mixed + et * dt
            inverse = 1.0 / jnp.sum(norm, axis=0, keepdims=True)
            delta = jnp.sum(mixed, axis=0, keepdims=True) * inverse
            for t, (et, dt) in enumerate(zip(e, d)):
                p = et * inverse
                ds = p * (dt - delta)
                if t == 0:
                    p_s[2 * BLK:3 * BLK, cols] = jnp.where(current, p, 0.0).astype(jnp.bfloat16)
                    p_s[0:BLK, cols] = jnp.where(current, 0.0, p).astype(jnp.bfloat16)
                    ds_s[2 * BLK:3 * BLK, cols] = jnp.where(current, ds, 0.0).astype(jnp.bfloat16)
                    ds_s[0:BLK, cols] = jnp.where(current, 0.0, ds).astype(jnp.bfloat16)
                else:
                    place = BLK if t == 1 else (t + 1) * BLK
                    p_s[place:place + BLK, cols] = p.astype(jnp.bfloat16)
                    ds_s[place:place + BLK, cols] = ds.astype(jnp.bfloat16)
        q_rows = jnp.concatenate([q_ref[:, h * HEAD_SIZE:(h + 1) * HEAD_SIZE] for h in range(REP)], axis=0)
        dk = dot(ds_s[0:total], q_rows) * FACTOR
        o_rows = jnp.concatenate([o_ref[:, h * HEAD_SIZE:(h + 1) * HEAD_SIZE] for h in range(REP)], axis=0)
        dv = dot(p_s[0:total], o_rows)
        near_acc[pl.ds(row, 3 * BLK), 0:HEAD_SIZE] += dk[0:3 * BLK]
        near_acc[pl.ds(row, 3 * BLK), HEAD_SIZE:] += dv[0:3 * BLK]
        for s in range(n):
            far_acc[pl.ds(slots[s], BLK), 0:HEAD_SIZE] += dk[(3 + s) * BLK:(4 + s) * BLK]
            far_acc[pl.ds(slots[s], BLK), HEAD_SIZE:] += dv[(3 + s) * BLK:(4 + s) * BLK]
        dqt = dot(kcat[0:total].T, ds_s[0:total]) * FACTOR
        for h in range(REP):
            cols = slice(h * HEAD_SIZE, (h + 1) * HEAD_SIZE)
            dq_ref[:, cols] = dqt[:, cols].T.astype(jnp.bfloat16)

    for n in range(LINKS + 1):
        pl.when(live == n)(functools.partial(work, n))

    @pl.when(b == block_count - 1)
    def _():
        near_ref[...] = near_acc[...]
        far_ref[...] = far_acc[...].astype(jnp.bfloat16)


def group_grads(chunk, links, header_blocks, index, queries, out_grad, extended, table, dq_prev):
    rows = queries.shape[0]
    block_count = rows // BLK
    groups = KEY_VALUE_HEADS // CHUNKS
    base = chunk * groups
    near_rows = extended.shape[0]
    far_rows = table.shape[0]
    wide = REP * HEAD_SIZE
    spec = lambda shape, f: pl.BlockSpec(shape, f)
    in_specs = [
        spec((BLK, wide), lambda g, b, *_: (b, base + g)),
        spec((BLK, wide), lambda g, b, *_: (b, base + g)),
        spec((near_rows, HEAD_SIZE), lambda g, b, *_: (0, base + g)),
        spec((near_rows, HEAD_SIZE), lambda g, b, *_: (0, KEY_VALUE_HEADS + base + g)),
        spec((far_rows, HEAD_SIZE), lambda g, b, *_: (0, g)),
        spec((far_rows, HEAD_SIZE), lambda g, b, *_: (0, groups + g)),
        pl.BlockSpec(memory_space=pl.ANY),
    ]
    args = [queries, out_grad, extended, extended, table, table]
    kernel = functools.partial(grad_kernel, block_count)
    aliases = {}
    if dq_prev is None:
        in_specs.pop()
        inner = kernel
        kernel = lambda *r: inner(*r[:9], None, *r[9:])
    else:
        args.append(dq_prev)
        aliases = {9: 0}
    span = (3 + LINKS) * BLK
    return pl.pallas_call(
        kernel,
        grid_spec=pltpu.PrefetchScalarGridSpec(
            num_scalar_prefetch=3,
            grid=(groups, block_count),
            in_specs=in_specs,
            out_specs=[
                spec((BLK, wide), lambda g, b, *_: (b, base + g)),
                spec((near_rows, 2 * HEAD_SIZE), lambda g, b, *_: (0, g)),
                spec((far_rows, 2 * HEAD_SIZE), lambda g, b, *_: (0, g)),
            ],
            scratch_shapes=[
                pltpu.VMEM((span, HEAD_SIZE), jnp.bfloat16),
                pltpu.VMEM((span, HEAD_SIZE), jnp.bfloat16),
                pltpu.VMEM((span, wide), jnp.bfloat16),
                pltpu.VMEM((span, wide), jnp.bfloat16),
                pltpu.VMEM((near_rows, 2 * HEAD_SIZE), jnp.float32),
                pltpu.VMEM((far_rows, 2 * HEAD_SIZE), jnp.float32),
            ],
        ),
        out_shape=[
            jax.ShapeDtypeStruct((rows, QUERY_HEADS * HEAD_SIZE), jnp.bfloat16),
            jax.ShapeDtypeStruct((near_rows, groups * 2 * HEAD_SIZE), jnp.float32),
            jax.ShapeDtypeStruct((far_rows, groups * 2 * HEAD_SIZE), jnp.bfloat16),
        ],
        input_output_aliases=aliases,
        compiler_params=pltpu.CompilerParams(dimension_semantics=("arbitrary", "arbitrary")),
        cost_estimate=pl.CostEstimate(flops=16_000_000_000 // CHUNKS, bytes_accessed=16_000_000 // CHUNKS,
                                      transcendentals=13_000_000 // CHUNKS),
        name="link_grads",
    )(links, header_blocks, index, *args)


def body(queries, keys, values, out_grad, links, header_blocks):
    rows = queries.shape[0]
    block_count = rows // BLK
    half = keys.shape[1]
    me = lax.axis_index("ctx")
    index = me.astype(jnp.int32).reshape(1)
    kv = jnp.concatenate([keys, values], axis=1)
    is_mine = header_blocks // block_count == me
    offset = jnp.sum(jnp.where(is_mine, header_blocks % block_count, 0)).astype(jnp.int32)
    holds = jnp.any(is_mine)
    slot = lax.dynamic_slice_in_dim(kv, offset * BLK, BLK, 0)
    width = half // CHUNKS
    tables = [
        lax.all_gather(
            jnp.concatenate([slot[:, c * width:(c + 1) * width], slot[:, half + c * width:half + (c + 1) * width]], axis=1),
            "ctx", axis=0, tiled=True)
        for c in range(CHUNKS)
    ]
    extended = jnp.concatenate([shifted(kv[rows - WIN:], "ctx", 1), kv], axis=0)
    peers = tables[0].shape[0] // BLK
    dq, key_parts, value_parts = None, [], []
    for c in range(CHUNKS):
        dq, near, far = group_grads(c, links, header_blocks, index, queries, out_grad, extended, tables[c], dq)
        back = shifted(near[:WIN].astype(jnp.bfloat16), "ctx", -1)
        own = lax.psum_scatter(far, "ctx", scatter_dimension=0, tiled=True)
        mask = (jnp.arange(block_count) == offset) & holds
        own = jnp.where(mask[:, None, None], own.astype(jnp.float32)[None], 0.0).reshape(rows, -1)
        local = near[WIN:] + own + jnp.pad(back.astype(jnp.float32), ((rows - WIN, 0), (0, 0)))
        local = local.reshape(rows, -1, 2, HEAD_SIZE)
        key_parts.append(local[:, :, 0].reshape(rows, -1))
        value_parts.append(local[:, :, 1].reshape(rows, -1))
    return dq, jnp.concatenate(key_parts, axis=1), jnp.concatenate(value_parts, axis=1)


def solution(mesh):
    row = P(("groups", "ctx"), None)
    return jax.shard_map(body, mesh=mesh, in_specs=(row, row, row, row, row, P("groups")),
                         out_specs=(row, row, row), check_vma=False)
```

```python
import functools
import math

import jax
import jax.numpy as jnp
from jax import lax
from jax.experimental import pallas as pl
from jax.experimental.pallas import tpu as pltpu
from jax.sharding import PartitionSpec as P

QUERY_HEADS = 28
KEY_VALUE_HEADS = 4
HEAD_SIZE = 128
BLK = 128
WIN = 256
LINKS = 4
REP = QUERY_HEADS // KEY_VALUE_HEADS
CHUNKS = 1
FACTOR = float(HEAD_SIZE) ** (-0.5)
EXP2_FACTOR = FACTOR * math.log2(math.e)
NT = (((1,), (1,)), ((), ()))


def shifted(x, axis, by):
    peers = lax.axis_size(axis)
    pairs = [(i, i + by) for i in range(peers) if 0 <= i + by < peers]
    return lax.ppermute(x, axis, pairs)


def halving_sum(table, axis, rows):
    peers = lax.axis_size(axis)
    me = lax.axis_index(axis)
    part = table.reshape(peers, rows, -1)
    step = 1
    while step < peers:
        pairs = part.reshape(part.shape[0] // 2, 2, rows, -1)
        bit = (me // step) % 2
        kept = lax.dynamic_index_in_dim(pairs, bit, 1, keepdims=False)
        sent = lax.dynamic_index_in_dim(pairs, 1 - bit, 1, keepdims=False)
        got = lax.ppermute(sent, axis, [(i, i ^ step) for i in range(peers)])
        part = kept.astype(jnp.float32) + got.astype(jnp.float32)
        step *= 2
        if step < peers:
            part = part.astype(jnp.bfloat16)
    return part.reshape(rows, -1)


def dot(a, b, dims=(((1,), (0,)), ((), ()))):
    return lax.dot_general(a, b, dims, preferred_element_type=jnp.float32)


def grad_kernel(block_count, links, headers, index, q_ref, o_ref, k_ref, v_ref, hk_ref, hv_ref, prev_ref,
                dq_ref, near_ref, far_ref, kcat, vcat, ds_s, p_s, near_acc, far_acc):
    b = pl.program_id(1)
    first = index[0] * block_count + b
    row = pl.multiple_of(b * BLK, BLK)

    @pl.when(b == 0)
    def _():
        near_acc[...] = jnp.zeros_like(near_acc)
        far_acc[...] = jnp.zeros_like(far_acc)

    kcat[0:3 * BLK] = k_ref[pl.ds(row, 3 * BLK), :]
    vcat[0:3 * BLK] = v_ref[pl.ds(row, 3 * BLK), :]
    live = jnp.int32(0)
    slots = [jnp.int32(0)] * LINKS
    for l in range(LINKS):
        entry = links[b, l]
        holder = headers[jnp.maximum(entry, 0)] // block_count
        for s in range(l + 1):
            slots[s] = jnp.where((entry >= 0) & (live == s), holder, slots[s])
        live = live + jnp.where(entry >= 0, 1, 0).astype(jnp.int32)
    slots = [pl.multiple_of(s * BLK, BLK) for s in slots]

    key_at = lax.broadcasted_iota(jnp.int32, (BLK, BLK), 0)
    query_at = lax.broadcasted_iota(jnp.int32, (BLK, BLK), 1)
    current = key_at <= query_at
    bias0 = jnp.where(first >= 2, 0.0, -1e30).astype(jnp.float32)
    bias1 = jnp.where(first >= 1, 0.0, -1e30).astype(jnp.float32)

    def work(n):
        for s in range(n):
            kcat[(3 + s) * BLK:(4 + s) * BLK] = hk_ref[pl.ds(slots[s], BLK), :]
            vcat[(3 + s) * BLK:(4 + s) * BLK] = hv_ref[pl.ds(slots[s], BLK), :]
        total = (3 + n) * BLK
        for h in range(REP):
            cols = slice(h * HEAD_SIZE, (h + 1) * HEAD_SIZE)
            st = dot(kcat[0:total], q_ref[:, cols], NT)
            dpt = dot(vcat[0:total], o_ref[:, cols], NT)
            x = [jnp.where(current, st[2 * BLK:3 * BLK], st[0:BLK] + bias0), st[BLK:2 * BLK] + bias1]
            d = [jnp.where(current, dpt[2 * BLK:3 * BLK], dpt[0:BLK]), dpt[BLK:2 * BLK]]
            for s in range(n):
                x.append(st[(3 + s) * BLK:(4 + s) * BLK])
                d.append(dpt[(3 + s) * BLK:(4 + s) * BLK])
            top = x[0]
            for t in x[1:]:
                top = jnp.maximum(top, t)
            top = jnp.max(top, axis=0, keepdims=True)
            e = [jnp.exp2((t - top) * EXP2_FACTOR) for t in x]
            norm = e[0]
            mixed = e[0] * d[0]
            for et, dt in zip(e[1:], d[1:]):
                norm = norm + et
                mixed = mixed + et * dt
            inverse = 1.0 / jnp.sum(norm, axis=0, keepdims=True)
            delta = jnp.sum(mixed, axis=0, keepdims=True) * inverse
            for t, (et, dt) in enumerate(zip(e, d)):
                p = et * inverse
                ds = p * (dt - delta)
                if t == 0:
                    p_s[2 * BLK:3 * BLK, cols] = jnp.where(current, p, 0.0).astype(jnp.bfloat16)
                    p_s[0:BLK, cols] = jnp.where(current, 0.0, p).astype(jnp.bfloat16)
                    ds_s[2 * BLK:3 * BLK, cols] = jnp.where(current, ds, 0.0).astype(jnp.bfloat16)
                    ds_s[0:BLK, cols] = jnp.where(current, 0.0, ds).astype(jnp.bfloat16)
                else:
                    place = BLK if t == 1 else (t + 1) * BLK
                    p_s[place:place + BLK, cols] = p.astype(jnp.bfloat16)
                    ds_s[place:place + BLK, cols] = ds.astype(jnp.bfloat16)
        q_rows = jnp.concatenate([q_ref[:, h * HEAD_SIZE:(h + 1) * HEAD_SIZE] for h in range(REP)], axis=0)
        dk = dot(ds_s[0:total], q_rows) * FACTOR
        o_rows = jnp.concatenate([o_ref[:, h * HEAD_SIZE:(h + 1) * HEAD_SIZE] for h in range(REP)], axis=0)
        dv = dot(p_s[0:total], o_rows)
        near_acc[pl.ds(row, 3 * BLK), 0:HEAD_SIZE] += dk[0:3 * BLK]
        near_acc[pl.ds(row, 3 * BLK), HEAD_SIZE:] += dv[0:3 * BLK]
        for s in range(n):
            far_acc[pl.ds(slots[s], BLK), 0:HEAD_SIZE] += dk[(3 + s) * BLK:(4 + s) * BLK]
            far_acc[pl.ds(slots[s], BLK), HEAD_SIZE:] += dv[(3 + s) * BLK:(4 + s) * BLK]
        dqt = dot(kcat[0:total].T, ds_s[0:total]) * FACTOR
        for h in range(REP):
            cols = slice(h * HEAD_SIZE, (h + 1) * HEAD_SIZE)
            dq_ref[:, cols] = dqt[:, cols].T.astype(jnp.bfloat16)

    for n in range(LINKS + 1):
        pl.when(live == n)(functools.partial(work, n))

    @pl.when(b == block_count - 1)
    def _():
        near_ref[...] = near_acc[...]
        far_ref[...] = far_acc[...].astype(jnp.bfloat16)


def group_grads(chunk, links, header_blocks, index, queries, out_grad, extended, table, dq_prev):
    rows = queries.shape[0]
    block_count = rows // BLK
    groups = KEY_VALUE_HEADS // CHUNKS
    base = chunk * groups
    near_rows = extended.shape[0]
    far_rows = table.shape[0]
    wide = REP * HEAD_SIZE
    spec = lambda shape, f: pl.BlockSpec(shape, f)
    in_specs = [
        spec((BLK, wide), lambda g, b, *_: (b, base + g)),
        spec((BLK, wide), lambda g, b, *_: (b, base + g)),
        spec((near_rows, HEAD_SIZE), lambda g, b, *_: (0, base + g)),
        spec((near_rows, HEAD_SIZE), lambda g, b, *_: (0, KEY_VALUE_HEADS + base + g)),
        spec((far_rows, HEAD_SIZE), lambda g, b, *_: (0, g)),
        spec((far_rows, HEAD_SIZE), lambda g, b, *_: (0, groups + g)),
        pl.BlockSpec(memory_space=pl.ANY),
    ]
    args = [queries, out_grad, extended, extended, table, table]
    kernel = functools.partial(grad_kernel, block_count)
    aliases = {}
    if dq_prev is None:
        in_specs.pop()
        inner = kernel
        kernel = lambda *r: inner(*r[:9], None, *r[9:])
    else:
        args.append(dq_prev)
        aliases = {9: 0}
    span = (3 + LINKS) * BLK
    return pl.pallas_call(
        kernel,
        grid_spec=pltpu.PrefetchScalarGridSpec(
            num_scalar_prefetch=3,
            grid=(groups, block_count),
            in_specs=in_specs,
            out_specs=[
                spec((BLK, wide), lambda g, b, *_: (b, base + g)),
                spec((near_rows, 2 * HEAD_SIZE), lambda g, b, *_: (0, g)),
                spec((far_rows, 2 * HEAD_SIZE), lambda g, b, *_: (0, g)),
            ],
            scratch_shapes=[
                pltpu.VMEM((span, HEAD_SIZE), jnp.bfloat16),
                pltpu.VMEM((span, HEAD_SIZE), jnp.bfloat16),
                pltpu.VMEM((span, wide), jnp.bfloat16),
                pltpu.VMEM((span, wide), jnp.bfloat16),
                pltpu.VMEM((near_rows, 2 * HEAD_SIZE), jnp.float32),
                pltpu.VMEM((far_rows, 2 * HEAD_SIZE), jnp.float32),
            ],
        ),
        out_shape=[
            jax.ShapeDtypeStruct((rows, QUERY_HEADS * HEAD_SIZE), jnp.bfloat16),
            jax.ShapeDtypeStruct((near_rows, groups * 2 * HEAD_SIZE), jnp.float32),
            jax.ShapeDtypeStruct((far_rows, groups * 2 * HEAD_SIZE), jnp.bfloat16),
        ],
        input_output_aliases=aliases,
        compiler_params=pltpu.CompilerParams(dimension_semantics=("arbitrary", "arbitrary")),
        cost_estimate=pl.CostEstimate(flops=16_000_000_000 // CHUNKS, bytes_accessed=16_000_000 // CHUNKS,
                                      transcendentals=13_000_000 // CHUNKS),
        name="link_grads",
    )(links, header_blocks, index, *args)


def body(queries, keys, values, out_grad, links, header_blocks):
    rows = queries.shape[0]
    block_count = rows // BLK
    half = keys.shape[1]
    me = lax.axis_index("ctx")
    index = me.astype(jnp.int32).reshape(1)
    kv = jnp.concatenate([keys, values], axis=1)
    is_mine = header_blocks // block_count == me
    offset = jnp.sum(jnp.where(is_mine, header_blocks % block_count, 0)).astype(jnp.int32)
    holds = jnp.any(is_mine)
    slot = lax.dynamic_slice_in_dim(kv, offset * BLK, BLK, 0)
    width = half // CHUNKS
    tables = [
        lax.all_gather(
            jnp.concatenate([slot[:, c * width:(c + 1) * width], slot[:, half + c * width:half + (c + 1) * width]], axis=1),
            "ctx", axis=0, tiled=True)
        for c in range(CHUNKS)
    ]
    extended = jnp.concatenate([shifted(kv[rows - WIN:], "ctx", 1), kv], axis=0)
    peers = tables[0].shape[0] // BLK
    dq, key_parts, value_parts = None, [], []
    for c in range(CHUNKS):
        dq, near, far = group_grads(c, links, header_blocks, index, queries, out_grad, extended, tables[c], dq)
        back = shifted(near[:WIN].astype(jnp.bfloat16), "ctx", -1)
        own = halving_sum(far, "ctx", BLK)
        mask = (jnp.arange(block_count) == offset) & holds
        own = jnp.where(mask[:, None, None], own.astype(jnp.float32)[None], 0.0).reshape(rows, -1)
        local = near[WIN:] + own + jnp.pad(back.astype(jnp.float32), ((rows - WIN, 0), (0, 0)))
        local = local.reshape(rows, -1, 2, HEAD_SIZE)
        key_parts.append(local[:, :, 0].reshape(rows, -1))
        value_parts.append(local[:, :, 1].reshape(rows, -1))
    return dq, jnp.concatenate(key_parts, axis=1), jnp.concatenate(value_parts, axis=1)


def solution(mesh):
    row = P(("groups", "ctx"), None)
    return jax.shard_map(body, mesh=mesh, in_specs=(row, row, row, row, row, P("groups")),
                         out_specs=(row, row, row), check_vma=False)
```
